32 devices in a mesh: seq: 8 (over z, x), doc: 4 (over y, core).
Axes of the slice: x: 2, y: 2, z: 4, core: 2. Of those that a mesh axis runs over, the one named last changes fastest.
Arguments:
- tokens: bfloat16 [16, 8192, 512], P('doc', 'seq'), may hold values from -6 to 6
- factor_one: bfloat16 [8, 1024, 1024], P('seq'), may hold values from -0.1875 to 0.1875
- factor_two: bfloat16 [1024, 8, 8], P('seq'), may hold values from -2 to 2
- gate_gain: float32 [512], replicated, may hold values from 0.5 to 2
- gate_bias: float32 [512], replicated, may hold values from -4 to 4
- block_counts: int32 [16], replicated, may hold values from 7 to 8, as said below
- partner: int32 [16], replicated, may hold values from 0 to 15, as said below
- reading: float32 [512, 256], replicated, may hold values from -0.25 to 0.25
Outputs:
- gated: bfloat16 [16, 8, 1024, 512], P('doc', None, 'seq')
- contrast: float32 [16, 256], P('doc')
The draws below stay inside these ranges and needn't reach their ends.
Inputs may be any that keep to these rules, and one draw needn't show every extreme that they name: `block_counts`: some document has all 8 blocks valid and another exactly 7. partner is a single cycle through all documents; no document is its own partner.
All inputs are finite; a program needn't handle non-finite values.
Results may differ from the reference program's by a relative error of at most 0.005.
Values may be sent and summed in bfloat16 or wider, within the bound.
A program may use at most 128 MiB of HBM per device.

```python
import jax
import jax.numpy as jnp
from jax import lax

BLK = 1024
C = 512
DIRS = 256
DOCS = 16
LEN = 8192
P_BLOCKS = 8


def draw_block_counts(key, part):
    key_a = jax.random.fold_in(key, 11)
    key_b = jax.random.fold_in(key, 12)
    key_c = jax.random.fold_in(key, 13)
    lowest = P_BLOCKS - P_BLOCKS // 8
    counts = jax.random.randint(key_a, (DOCS,), lowest, P_BLOCKS + 1)
    chosen = jax.random.randint(key_b, (), 0, DOCS)
    step_over = jax.random.randint(key_c, (), 1, DOCS)
    second = (chosen + step_over) % DOCS
    places = jnp.arange(DOCS)
    counts = jnp.where(places == chosen, P_BLOCKS, counts)
    counts = jnp.where(places == second, lowest, counts)
    return counts.astype(jnp.int32)


def draw_partner(key, part):
    order = jax.random.permutation(jax.random.fold_in(key, 21), DOCS).astype(jnp.int32)
    return jnp.zeros((DOCS,), jnp.int32).at[order].set(jnp.roll(order, -1))


def levels(own_key, extent, shards, least, top_value):
    level, own = 1.0, jax.random.fold_in(own_key, 6)
    for axis_at, blocks in shards:
        steps = jnp.exp(jax.random.uniform(jax.random.fold_in(own, axis_at), (blocks,), jnp.float32, least / len(shards), top_value / len(shards)))
        level = level * jnp.repeat(steps, extent[axis_at] // blocks).reshape([-1 if axis == axis_at else 1 for axis in range(len(extent))])
    return level


def bell_draw(rng, extent, width, limit, cuts=(), kind=jnp.bfloat16):
    entries = jax.random.normal(rng, extent, jnp.float32) * width
    if len(cuts) > 0:
        entries = levels(rng, extent, cuts, -0.22, 0.18) * entries
    return jnp.clip(entries, min=-limit, max=limit).astype(kind)


def setup_inputs(seed: int = 0) -> dict:
    keys = jax.random.split(jax.random.key(seed), 9)
    return {
        "tokens": bell_draw(keys[0], (DOCS, LEN, C), 1.0, 6.0, ((0, 4), (1, 8))),
        "factor_one": bell_draw(keys[1], (P_BLOCKS, BLK, BLK), BLK ** -0.5, 0.1875, ((0, 8),)),
        "factor_two": bell_draw(keys[2], (BLK, P_BLOCKS, P_BLOCKS), P_BLOCKS ** -0.5, 2.0, ((0, 8),)),
        "gate_gain": jnp.clip(jax.random.uniform(keys[3], (C,), jnp.float32, 0.5, 2.0), 0.5, 2.0),
        "gate_bias": bell_draw(keys[4], (C,), 1.0, 4.0, (), jnp.float32),
        "block_counts": draw_block_counts(jax.random.fold_in(keys[8], 71), 0),
        "partner": draw_partner(jax.random.fold_in(keys[8], 71), 0),
        "reading": bell_draw(keys[7], (C, DIRS), C ** -0.5, 0.25, (), jnp.float32),
    }


def reference(tokens, factor_one, factor_two, gate_gain, gate_bias, block_counts, partner, reading):
    grid_all = tokens.reshape(DOCS, P_BLOCKS, BLK, C)
    first = factor_one.astype(jnp.float32)
    second_w = factor_two.astype(jnp.float32)
    rows = jnp.arange(P_BLOCKS, dtype=jnp.int32)

    def one_doc(item):
        grid, count = item
        keep = rows < count
        grid = grid * keep.astype(jnp.bfloat16)[:, None, None]
        mixed = jnp.einsum('pic,pij->pjc', grid.astype(jnp.float32), first).astype(jnp.bfloat16)
        second = jnp.einsum('pjc,jpq->qjc', mixed.astype(jnp.float32), second_w)
        gate = jax.nn.sigmoid(gate_gain * grid.astype(jnp.float32) + gate_bias)
        full = second * gate
        total = lax.optimization_barrier(jnp.sum(full * keep.astype(jnp.float32)[:, None, None], axis=(0, 1)))
        pooled = total / jnp.sqrt(count.astype(jnp.float32) * BLK)
        return (full.astype(jnp.bfloat16), pooled)
    gated, pooled = lax.map(one_doc, (grid_all, block_counts))
    other = pooled[partner]
    contrast = jnp.dot(pooled - other, reading, precision=lax.Precision.HIGHEST)
    return (gated, contrast)
```

```python
import functools

import jax
import jax.numpy as jnp
from jax import lax
from jax.experimental import pallas as pl
from jax.experimental.pallas import tpu as pltpu
from jax.sharding import PartitionSpec as P

F32 = jnp.float32
BF16 = jnp.bfloat16
MESH = pl.DeviceIdType.MESH


def mixer_kernel(
    n,
    m,
    counts,
    partner,
    tokens,
    f1_hbm,
    f2,
    gain,
    bias,
    reading,
    gated,
    contrast,
    tok,
    f1,
    mixed,
    vals,
    inps,
    w,
    outs,
    part,
    pbuf,
    gbuf,
    local_sem,
    out_sem,
    isend,
    irecv,
    vsend,
    vrecv,
    psend,
    precv,
    gsend,
    grecv,
):
    docs, blk, chan = tokens.shape
    rows = blk // n
    me = lax.axis_index("seq")
    my_doc = lax.axis_index("doc")
    doc_start = my_doc * docs

    def peer(k):
        return lax.rem(me + k, n)

    def doc_peer(k):
        return lax.rem(my_doc + k, m)

    load_tok = pltpu.make_async_copy(tokens, tok, local_sem.at[0])
    load_f1 = pltpu.make_async_copy(f1_hbm.at[0], f1, local_sem.at[1])
    own_slice = pl.ds(pl.multiple_of(me * rows, rows), rows)
    own_in = pltpu.make_async_copy(
        tokens.at[:, own_slice], inps.at[:, own_slice], local_sem.at[2]
    )
    load_tok.start()
    load_f1.start()
    own_in.start()

    barrier = pltpu.get_barrier_semaphore()
    for k in range(1, n):
        pl.semaphore_signal(barrier, inc=1, device_id={"seq": peer(k)}, device_id_type=MESH)
    for k in range(1, m):
        pl.semaphore_signal(barrier, inc=1, device_id={"doc": doc_peer(k)}, device_id_type=MESH)
    pl.semaphore_wait(barrier, n - 1 + m - 1)

    order = sorted(range(1, n), key=lambda k: abs(k - n // 2))
    sends_in = []
    for k in order:
        theirs = pl.ds(pl.multiple_of(peer(k) * rows, rows), rows)
        copy = pltpu.make_async_remote_copy(
            src_ref=tokens.at[:, theirs],
            dst_ref=inps.at[:, own_slice],
            send_sem=isend.at[k],
            recv_sem=irecv.at[k],
            device_id={"seq": peer(k)},
            device_id_type=MESH,
        )
        copy.start()
        sends_in.append(copy)

    load_tok.wait()
    load_f1.wait()
    tile = 256
    sends_val = []
    for d in range(docs):
        keep = (counts[doc_start + d] > me).astype(F32)

        @pl.loop(0, blk // tile)
        def _(t):
            cols = pl.ds(pl.multiple_of(t * tile, tile), tile)
            acc = lax.dot_general(
                f1[:, cols],
                tok[d],
                (((0,), (0,)), ((), ())),
                preferred_element_type=F32,
            )
            mixed[d, cols, :] = (acc * keep).astype(BF16)

        for k in order:
            theirs = pl.ds(pl.multiple_of(peer(k) * rows, rows), rows)
            copy = pltpu.make_async_remote_copy(
                src_ref=mixed.at[d, theirs],
                dst_ref=vals.at[d, own_slice],
                send_sem=vsend.at[d, k],
                recv_sem=vrecv.at[d, k],
                device_id={"seq": peer(k)},
                device_id_type=MESH,
            )
            copy.start()
            sends_val.append(copy)
        vals[d, own_slice, :] = mixed[d, own_slice, :]

    eye = lax.broadcasted_iota(jnp.int32, (rows, rows), 0) == lax.broadcasted_iota(
        jnp.int32, (rows, rows), 1
    )
    for p in range(n):
        for q in range(n):
            line = f2[p, q : q + 1, :].astype(F32)
            w[q * rows : (q + 1) * rows, p * rows : (p + 1) * rows] = jnp.where(
                eye, line, 0.0
            ).astype(BF16)

    own_in.wait()
    for copy in sends_in:
        copy.wait_recv()

    writes = []
    for d in range(docs):
        for copy in sends_val[d * (n - 1) : (d + 1) * (n - 1)]:
            copy.wait_recv()
        count = counts[doc_start + d]
        part[d : d + 1, :] = jnp.zeros((1, chan), F32)

        @pl.loop(0, n // 2)
        def _(pair):
            two = pl.ds(pl.multiple_of(pair * 2 * rows, 2 * rows), 2 * rows)
            second = jnp.dot(w[two, :], vals[d], preferred_element_type=F32)
            for h in range(2):
                q = pair * 2 + h
                keep = (q < count).astype(F32)
                here = pl.ds(pl.multiple_of(q * rows, rows), rows)
                grid = inps[d, here, :].astype(F32) * keep
                gate = 1.0 / (1.0 + jnp.exp(-(gain[...] * grid + bias[...])))
                full = second[h * rows : (h + 1) * rows] * gate
                outs[d, here, :] = full.astype(BF16)
                part[d : d + 1, :] += jnp.sum(full, axis=0, keepdims=True) * keep

        write = pltpu.make_async_copy(outs.at[d], gated.at[d], out_sem.at[d])
        write.start()
        writes.append(write)

    small = []
    for k in range(1, n):
        copy = pltpu.make_async_remote_copy(
            src_ref=part,
            dst_ref=pbuf.at[me],
            send_sem=psend.at[k],
            recv_sem=precv.at[k],
            device_id={"seq": peer(k)},
            device_id_type=MESH,
        )
        copy.start()
        small.append(copy)
    pbuf[me] = part[...]
    for copy in small:
        copy.wait_recv()
    total = pbuf[0]
    for p in range(1, n):
        total = total + pbuf[p]
    mine = []
    for d in range(docs):
        size = jnp.full((1, chan), counts[doc_start + d], jnp.int32).astype(F32) * blk
        mine.append(total[d : d + 1] / jnp.sqrt(size))
    mine = jnp.concatenate(mine, axis=0)
    gbuf[my_doc] = mine
    for k in range(1, m):
        copy = pltpu.make_async_remote_copy(
            src_ref=gbuf.at[my_doc],
            dst_ref=gbuf.at[my_doc],
            send_sem=gsend.at[k],
            recv_sem=grecv.at[k],
            device_id={"doc": doc_peer(k)},
            device_id_type=MESH,
        )
        copy.start()
        small.append(copy)
    for copy in small[n - 1 :]:
        copy.wait_recv()
    others = []
    for d in range(docs):
        want = partner[doc_start + d]
        other = jnp.zeros((1, chan), F32)
        for e in range(m * docs):
            pick = (want == e).astype(F32)
            other = other + gbuf[e // docs, e % docs : e % docs + 1, :] * pick
        others.append(other)
    diff = mine - jnp.concatenate(others, axis=0)
    contrast[...] = jnp.dot(
        diff, reading[...], precision=lax.Precision.HIGHEST, preferred_element_type=F32
    )

    for copy in sends_in + sends_val + small:
        copy.wait_send()
    for write in writes:
        write.wait()


def fused(n, m, tokens, factor_one, factor_two, gate_gain, gate_bias, block_counts, partner, reading):
    docs, blk, chan = tokens.shape
    dirs = reading.shape[1]
    smem = pl.BlockSpec(memory_space=pltpu.SMEM)
    vmem = pl.BlockSpec(memory_space=pltpu.VMEM)
    hbm = pl.BlockSpec(memory_space=pl.ANY)
    dma = pltpu.SemaphoreType.DMA
    rows = blk // n
    gated, contrast = pl.pallas_call(
        functools.partial(mixer_kernel, n, m),
        out_shape=(
            jax.ShapeDtypeStruct((docs, blk, chan), BF16),
            jax.ShapeDtypeStruct((docs, dirs), F32),
        ),
        in_specs=[smem, smem, hbm, hbm, vmem, vmem, vmem, vmem],
        out_specs=(hbm, vmem),
        scratch_shapes=[
            pltpu.VMEM((docs, blk, chan), BF16),
            pltpu.VMEM((blk, blk), BF16),
            pltpu.VMEM((docs, blk, chan), BF16),
            pltpu.VMEM((docs, blk, chan), BF16),
            pltpu.VMEM((docs, blk, chan), BF16),
            pltpu.VMEM((blk, blk), BF16),
            pltpu.VMEM((docs, blk, chan), BF16),
            pltpu.VMEM((docs, chan), F32),
            pltpu.VMEM((n, docs, chan), F32),
            pltpu.VMEM((m, docs, chan), F32),
            dma((3,)),
            dma((docs,)),
            dma((n,)),
            dma((n,)),
            dma((docs, n)),
            dma((docs, n)),
            dma((n,)),
            dma((n,)),
            dma((m,)),
            dma((m,)),
        ],
        compiler_params=pltpu.CompilerParams(
            collective_id=0, has_side_effects=True, vmem_limit_bytes=56 << 20
        ),
        name="mixer",
    )(
        block_counts,
        partner,
        tokens,
        factor_one,
        jnp.transpose(factor_two, (1, 2, 0)),
        gate_gain[None, :],
        gate_bias[None, :],
        reading,
    )
    return gated.reshape(docs, n, rows, chan), contrast


def plain(tokens, factor_one, factor_two, gate_gain, gate_bias, block_counts, partner, reading):
    doc_dev, _, chan = tokens.shape
    blocks_dev, blk_size = (factor_one.shape[0], factor_one.shape[1])
    all_blocks = factor_two.shape[1]
    all_docs = block_counts.shape[0]
    doc_start = lax.axis_index("doc") * doc_dev
    block_start = lax.axis_index("seq") * blocks_dev
    local_counts = lax.dynamic_slice_in_dim(block_counts, doc_start, doc_dev)
    block_ids = block_start + jnp.arange(blocks_dev, dtype=jnp.int32)
    inside = (block_ids[None, :] < local_counts[:, None]).astype(BF16)
    grid = tokens.reshape(doc_dev, blocks_dev, blk_size, chan) * inside[:, :, None, None]
    mixed = jnp.einsum("dbic,bij->dbjc", grid, factor_one, preferred_element_type=F32).astype(BF16)
    values_t = lax.all_to_all(mixed, "seq", split_axis=2, concat_axis=1, tiled=True)
    inputs_t = lax.all_to_all(grid, "seq", split_axis=2, concat_axis=1, tiled=True)
    second = jnp.einsum("dpjc,jpq->dqjc", values_t, factor_two, preferred_element_type=F32)
    full = second * jax.nn.sigmoid(gate_gain * inputs_t.astype(F32) + gate_bias)
    keep = (jnp.arange(all_blocks, dtype=jnp.int32)[None, :] < local_counts[:, None]).astype(F32)
    partial_value = jnp.sum(full * keep[:, :, None, None], axis=(1, 2))
    scale = 1.0 / jnp.sqrt(local_counts.astype(F32) * blk_size)
    mine = lax.psum(partial_value, "seq") * scale[:, None]
    pooled_all = lax.all_gather(mine, "doc", axis=0, tiled=True)
    local_partner = lax.dynamic_slice_in_dim(partner, doc_start, doc_dev)
    picker = (local_partner[:, None] == jnp.arange(all_docs, dtype=jnp.int32)[None, :]).astype(F32)
    other = jnp.dot(picker, pooled_all, precision=lax.Precision.HIGHEST)
    contrast = jnp.dot(mine - other, reading, precision=lax.Precision.HIGHEST)
    return full.astype(BF16), contrast


def solution(mesh):
    n, m = mesh.shape["seq"], mesh.shape["doc"]

    def shards(*args):
        factor_one, factor_two = args[1], args[2]
        lanes = factor_two.shape[0] % 128 == 0
        if factor_one.shape[0] == 1 and factor_two.shape[1] == n and n % 2 == 0 and lanes:
            return fused(n, m, *args)
        return plain(*args)

    placed = (
        P("doc", "seq", None),
        P("seq", None, None),
        P("seq", None, None),
        P(),
        P(),
        P(),
        P(),
        P(),
    )
    return jax.shard_map(
        shards,
        mesh=mesh,
        in_specs=placed,
        out_specs=(P("doc", None, "seq", None), P("doc", None)),
        check_vma=False,
    )
```

```python
import functools

import jax
import jax.numpy as jnp
from jax import lax
from jax.experimental import pallas as pl
from jax.experimental.pallas import tpu as pltpu
from jax.sharding import PartitionSpec as P

F32 = jnp.float32
BF16 = jnp.bfloat16
MESH = pl.DeviceIdType.MESH


def mixer_kernel(
    n,
    m,
    counts,
    tokens,
    f1_hbm,
    f2_hbm,
    gain_hbm,
    bias_hbm,
    gated,
    gbuf,
    tok,
    f1,
    mixed,
    vals,
    inps,
    w,
    part,
    pbuf,
    gates,
    f2,
    gain,
    bias,
    local_sem,
    isend,
    irecv,
    vsend,
    vrecv,
    psend,
    precv,
    gsend,
    grecv,
):
    docs, blk, chan = tokens.shape
    rows = blk // n
    me = lax.axis_index("seq")
    my_doc = lax.axis_index("doc")
    doc_start = my_doc * docs

    def peer(k):
        return lax.rem(me + k, n)

    def doc_peer(k):
        return lax.rem(my_doc + k, m)

    load_tok = pltpu.make_async_copy(tokens, tok, local_sem.at[0])
    load_f1 = pltpu.make_async_copy(f1_hbm.at[0], f1, local_sem.at[1])
    own_slice = pl.ds(pl.multiple_of(me * rows, rows), rows)
    own_in = pltpu.make_async_copy(
        tokens.at[:, own_slice], inps.at[:, own_slice], local_sem.at[2]
    )
    tables = [
        pltpu.make_async_copy(src, dst, local_sem.at[3 + i])
        for i, (src, dst) in enumerate(
            ((f2_hbm, f2), (gain_hbm, gain), (bias_hbm, bias))
        )
    ]

    barrier = pltpu.get_barrier_semaphore()
    for k in range(1, n):
        pl.semaphore_signal(barrier, inc=1, device_id={"seq": peer(k)}, device_id_type=MESH)
    for k in range(1, m):
        pl.semaphore_signal(barrier, inc=1, device_id={"doc": doc_peer(k)}, device_id_type=MESH)
    pl.semaphore_wait(barrier, n - 1 + m - 1)

    order = sorted(range(1, n), key=lambda k: abs(k - n // 2))
    sends_in = []
    for k in order:
        theirs = pl.ds(pl.multiple_of(peer(k) * rows, rows), rows)
        copy = pltpu.make_async_remote_copy(
            src_ref=tokens.at[:, theirs],
            dst_ref=inps.at[:, own_slice],
            send_sem=isend.at[k],
            recv_sem=irecv.at[k],
            device_id={"seq": peer(k)},
            device_id_type=MESH,
        )
        copy.start()
        sends_in.append(copy)

    load_tok.start()
    load_f1.start()
    own_in.start()
    for load in tables:
        load.start()
    load_tok.wait()
    load_f1.wait()
    tile = 256
    half = chan // 2
    pieces = [(d, 0, chan) for d in range(docs - 1)]
    pieces += [(docs - 1, 0, half), (docs - 1, half, half)]
    sends_val = []
    for d in range(docs):
        keep = (counts[doc_start + d] > me).astype(F32)

        @pl.loop(0, blk // tile)
        def _(t):
            cols = pl.ds(pl.multiple_of(t * tile, tile), tile)
            acc = lax.dot_general(
                f1[:, cols],
                tok[d],
                (((0,), (0,)), ((), ())),
                preferred_element_type=F32,
            )
            mixed[d, cols, :] = (acc * keep).astype(BF16)

        for i, (doc, start, width) in enumerate(pieces):
            if doc != d:
                continue
            lanes = pl.ds(start, width)
            for k in order:
                theirs = pl.ds(pl.multiple_of(peer(k) * rows, rows), rows)
                copy = pltpu.make_async_remote_copy(
                    src_ref=mixed.at[d, theirs, lanes],
                    dst_ref=vals.at[d, own_slice, lanes],
                    send_sem=vsend.at[i, k],
                    recv_sem=vrecv.at[i, k],
                    device_id={"seq": peer(k)},
                    device_id_type=MESH,
                )
                copy.start()
                sends_val.append(copy)
        vals[d, own_slice, :] = mixed[d, own_slice, :]

    for load in tables:
        load.wait()
    eye = lax.broadcasted_iota(jnp.int32, (rows, rows), 0) == lax.broadcasted_iota(
        jnp.int32, (rows, rows), 1
    )
    for p in range(n):
        for q in range(n):
            line = f2[p, q : q + 1, :].astype(F32)
            w[q * rows : (q + 1) * rows, p * rows : (p + 1) * rows] = jnp.where(
                eye, line, 0.0
            ).astype(BF16)

    own_in.wait()
    for copy in sends_in:
        copy.wait_recv()

    part[...] = jnp.zeros_like(part)
    for i, (d, start, width) in enumerate(pieces):
        count = counts[doc_start + d]
        lanes = pl.ds(start, width)
        if start == 0:

            @pl.loop(0, n)
            def _(q):
                here = pl.ds(pl.multiple_of(q * rows, rows), rows)
                grid = inps[d, here, :].astype(F32) * (q < count).astype(F32)
                gates[here, :] = 1.0 / (1.0 + jnp.exp(-(gain[...] * grid + bias[...])))

        for copy in sends_val[i * (n - 1) : (i + 1) * (n - 1)]:
            copy.wait_recv()

        @pl.loop(0, n // 2)
        def _(pair):
            two = pl.ds(pl.multiple_of(pair * 2 * rows, 2 * rows), 2 * rows)
            second = jnp.dot(w[two, :], vals[d, :, lanes], preferred_element_type=F32)
            full = second * gates[two, lanes]
            gated[d, two, lanes] = full.astype(BF16)
            for h in range(2):
                keep = (pair * 2 + h < count).astype(F32)
                line = jnp.sum(full[h * rows : (h + 1) * rows], axis=0, keepdims=True)
                part[d : d + 1, lanes] += line * keep

    small = []
    for k in range(1, n):
        copy = pltpu.make_async_remote_copy(
            src_ref=part,
            dst_ref=pbuf.at[me],
            send_sem=psend.at[k],
            recv_sem=precv.at[k],
            device_id={"seq": peer(k)},
            device_id_type=MESH,
        )
        copy.start()
        small.append(copy)
    pbuf[me] = part[...]
    for copy in small:
        copy.wait_recv()
    total = pbuf[0]
    for p in range(1, n):
        total = total + pbuf[p]
    mine = []
    for d in range(docs):
        size = jnp.full((1, chan), counts[doc_start + d], jnp.int32).astype(F32) * blk
        mine.append(total[d : d + 1] / jnp.sqrt(size))
    mine = jnp.concatenate(mine, axis=0)
    gbuf[my_doc] = mine
    for k in range(1, m):
        copy = pltpu.make_async_remote_copy(
            src_ref=gbuf.at[my_doc],
            dst_ref=gbuf.at[my_doc],
            send_sem=gsend.at[k],
            recv_sem=grecv.at[k],
            device_id={"doc": doc_peer(k)},
            device_id_type=MESH,
        )
        copy.start()
        small.append(copy)
    for copy in small[n - 1 :]:
        copy.wait_recv()
    for copy in sends_in + sends_val + small:
        copy.wait_send()


def finish_kernel(partner, held, pooled, reading_hbm, gated, contrast, reading, sem):
    m, docs, chan = pooled.shape
    load = pltpu.make_async_copy(reading_hbm, reading, sem.at[0])
    load.start()
    write = pltpu.make_async_copy(held, gated, sem.at[1])
    write.start()
    my_doc = lax.axis_index("doc")
    others = []
    for d in range(docs):
        want = partner[my_doc * docs + d]
        other = jnp.zeros((1, chan), F32)
        for e in range(m * docs):
            pick = (want == e).astype(F32)
            other = other + pooled[e // docs, e % docs : e % docs + 1, :] * pick
        others.append(other)
    diff = pooled[my_doc] - jnp.concatenate(others, axis=0)
    load.wait()
    contrast[...] = jnp.dot(
        diff, reading[...], precision=lax.Precision.HIGHEST, preferred_element_type=F32
    )
    write.wait()


def fused(n, m, tokens, factor_one, factor_two, gate_gain, gate_bias, block_counts, partner, reading):
    docs, blk, chan = tokens.shape
    dirs = reading.shape[1]
    smem = pl.BlockSpec(memory_space=pltpu.SMEM)
    vmem = pl.BlockSpec(memory_space=pltpu.VMEM)
    hbm = pl.BlockSpec(memory_space=pl.ANY)
    dma = pltpu.SemaphoreType.DMA
    rows = blk // n
    gated, pooled = pl.pallas_call(
        functools.partial(mixer_kernel, n, m),
        out_shape=(
            pltpu.VMEM((docs, blk, chan), BF16),
            pltpu.VMEM((m, docs, chan), F32),
        ),
        in_specs=[smem, hbm, hbm, hbm, hbm, hbm],
        out_specs=(vmem, vmem),
        scratch_shapes=[
            pltpu.VMEM((docs, blk, chan), BF16),
            pltpu.VMEM((blk, blk), BF16),
            pltpu.VMEM((docs, blk, chan), BF16),
            pltpu.VMEM((docs, blk, chan), BF16),
            pltpu.VMEM((docs, blk, chan), BF16),
            pltpu.VMEM((blk, blk), BF16),
            pltpu.VMEM((docs, chan), F32),
            pltpu.VMEM((n, docs, chan), F32),
            pltpu.VMEM((blk, chan), F32),
            pltpu.VMEM((n, n, rows), BF16),
            pltpu.VMEM((1, chan), F32),
            pltpu.VMEM((1, chan), F32),
            dma((6,)),
            dma((n,)),
            dma((n,)),
            dma((docs + 1, n)),
            dma((docs + 1, n)),
            dma((n,)),
            dma((n,)),
            dma((m,)),
            dma((m,)),
        ],
        compiler_params=pltpu.CompilerParams(
            collective_id=0, has_side_effects=True, vmem_limit_bytes=56 << 20
        ),
        name="mixer",
    )(
        block_counts,
        tokens,
        factor_one,
        jnp.transpose(factor_two, (1, 2, 0)),
        gate_gain[None, :],
        gate_bias[None, :],
    )
    gated, contrast = pl.pallas_call(
        finish_kernel,
        out_shape=(
            jax.ShapeDtypeStruct((docs, blk, chan), BF16),
            jax.ShapeDtypeStruct((docs, dirs), F32),
        ),
        in_specs=[smem, vmem, vmem, hbm],
        out_specs=(hbm, vmem),
        scratch_shapes=[pltpu.VMEM((chan, dirs), F32), dma((2,))],
        compiler_params=pltpu.CompilerParams(vmem_limit_bytes=16 << 20),
        name="finish",
    )(partner, gated, pooled, reading)
    return gated.reshape(docs, n, rows, chan), contrast


def plain(tokens, factor_one, factor_two, gate_gain, gate_bias, block_counts, partner, reading):
    doc_dev, _, chan = tokens.shape
    blocks_dev, blk_size = (factor_one.shape[0], factor_one.shape[1])
    all_blocks = factor_two.shape[1]
    all_docs = block_counts.shape[0]
    doc_start = lax.axis_index("doc") * doc_dev
    block_start = lax.axis_index("seq") * blocks_dev
    local_counts = lax.dynamic_slice_in_dim(block_counts, doc_start, doc_dev)
    block_ids = block_start + jnp.arange(blocks_dev, dtype=jnp.int32)
    inside = (block_ids[None, :] < local_counts[:, None]).astype(BF16)
    grid = tokens.reshape(doc_dev, blocks_dev, blk_size, chan) * inside[:, :, None, None]
    mixed = jnp.einsum("dbic,bij->dbjc", grid, factor_one, preferred_element_type=F32).astype(BF16)
    values_t = lax.all_to_all(mixed, "seq", split_axis=2, concat_axis=1, tiled=True)
    inputs_t = lax.all_to_all(grid, "seq", split_axis=2, concat_axis=1, tiled=True)
    second = jnp.einsum("dpjc,jpq->dqjc", values_t, factor_two, preferred_element_type=F32)
    full = second * jax.nn.sigmoid(gate_gain * inputs_t.astype(F32) + gate_bias)
    keep = (jnp.arange(all_blocks, dtype=jnp.int32)[None, :] < local_counts[:, None]).astype(F32)
    partial_value = jnp.sum(full * keep[:, :, None, None], axis=(1, 2))
    scale = 1.0 / jnp.sqrt(local_counts.astype(F32) * blk_size)
    mine = lax.psum(partial_value, "seq") * scale[:, None]
    pooled_all = lax.all_gather(mine, "doc", axis=0, tiled=True)
    local_partner = lax.dynamic_slice_in_dim(partner, doc_start, doc_dev)
    picker = (local_partner[:, None] == jnp.arange(all_docs, dtype=jnp.int32)[None, :]).astype(F32)
    other = jnp.dot(picker, pooled_all, precision=lax.Precision.HIGHEST)
    contrast = jnp.dot(mine - other, reading, precision=lax.Precision.HIGHEST)
    return full.astype(BF16), contrast


def solution(mesh):
    n, m = mesh.shape["seq"], mesh.shape["doc"]

    def shards(*args):
        factor_one, factor_two = args[1], args[2]
        lanes = factor_two.shape[0] % 128 == 0
        if factor_one.shape[0] == 1 and factor_two.shape[1] == n and n % 2 == 0 and lanes:
            return fused(n, m, *args)
        return plain(*args)

    placed = (
        P("doc", "seq", None),
        P("seq", None, None),
        P("seq", None, None),
        P(),
        P(),
        P(),
        P(),
        P(),
    )
    return jax.shard_map(
        shards,
        mesh=mesh,
        in_specs=placed,
        out_specs=(P("doc", None, "seq", None), P("doc", None)),
        check_vma=False,
    )
```

```python
import functools

import jax
import jax.numpy as jnp
from jax import lax
from jax.experimental import pallas as pl
from jax.experimental.pallas import tpu as pltpu
from jax.sharding import PartitionSpec as P

F32 = jnp.float32
BF16 = jnp.bfloat16
MESH = pl.DeviceIdType.MESH


def mixer_kernel(
    n,
    m,
    counts,
    tokens,
    f1_hbm,
    f2_hbm,
    gain_hbm,
    bias_hbm,
    gated,
    gbuf,
    tok,
    f1,
    mixed,
    vals,
    inps,
    w,
    part,
    pbuf,
    gates,
    scale,
    f2,
    gain,
    bias,
    local_sem,
    isend,
    irecv,
    vsend,
    vrecv,
    psend,
    precv,
    gsend,
    grecv,
):
    docs, blk, chan = tokens.shape
    rows = blk // n
    me = lax.axis_index("seq")
    my_doc = lax.axis_index("doc")
    doc_start = my_doc * docs

    def peer(k):
        return lax.rem(me + k, n)

    def doc_peer(k):
        return lax.rem(my_doc + k, m)

    load_tok = pltpu.make_async_copy(tokens, tok, local_sem.at[0])
    load_f1 = pltpu.make_async_copy(f1_hbm.at[0], f1, local_sem.at[1])
    own_slice = pl.ds(pl.multiple_of(me * rows, rows), rows)
    own_in = pltpu.make_async_copy(
        tokens.at[:, own_slice], inps.at[:, own_slice], local_sem.at[2]
    )
    tables = [
        pltpu.make_async_copy(src, dst, local_sem.at[3 + i])
        for i, (src, dst) in enumerate(
            ((f2_hbm, f2), (gain_hbm, gain), (bias_hbm, bias))
        )
    ]

    barrier = pltpu.get_barrier_semaphore()
    for k in range(1, n):
        pl.semaphore_signal(barrier, inc=1, device_id={"seq": peer(k)}, device_id_type=MESH)
    for k in range(1, m):
        pl.semaphore_signal(barrier, inc=1, device_id={"doc": doc_peer(k)}, device_id_type=MESH)
    pl.semaphore_wait(barrier, n - 1 + m - 1)

    order = sorted(range(1, n), key=lambda k: abs(k - n // 2))
    sends_in = []
    for k in order:
        theirs = pl.ds(pl.multiple_of(peer(k) * rows, rows), rows)
        copy = pltpu.make_async_remote_copy(
            src_ref=tokens.at[:, theirs],
            dst_ref=inps.at[:, own_slice],
            send_sem=isend.at[k],
            recv_sem=irecv.at[k],
            device_id={"seq": peer(k)},
            device_id_type=MESH,
        )
        copy.start()
        sends_in.append(copy)

    load_tok.start()
    load_f1.start()
    own_in.start()
    for load in tables:
        load.start()
    load_tok.wait()
    load_f1.wait()
    tile = 256
    half = chan // 2
    pieces = [(d, 0, chan) for d in range(docs - 1)]
    pieces += [(docs - 1, 0, half), (docs - 1, half, half)]
    sends_val = []
    for d in range(docs):
        keep = (counts[doc_start + d] > me).astype(F32)

        @pl.loop(0, blk // tile)
        def _(t):
            cols = pl.ds(pl.multiple_of(t * tile, tile), tile)
            acc = lax.dot_general(
                f1[:, cols],
                tok[d],
                (((0,), (0,)), ((), ())),
                preferred_element_type=F32,
            )
            mixed[d, cols, :] = (acc * keep).astype(BF16)

        for i, (doc, start, width) in enumerate(pieces):
            if doc != d:
                continue
            lanes = pl.ds(start, width)
            for k in order:
                theirs = pl.ds(pl.multiple_of(peer(k) * rows, rows), rows)
                copy = pltpu.make_async_remote_copy(
                    src_ref=mixed.at[d, theirs, lanes],
                    dst_ref=vals.at[d, own_slice, lanes],
                    send_sem=vsend.at[i, k],
                    recv_sem=vrecv.at[i, k],
                    device_id={"seq": peer(k)},
                    device_id_type=MESH,
                )
                copy.start()
                sends_val.append(copy)
        vals[d, own_slice, :] = mixed[d, own_slice, :]

    for load in tables:
        load.wait()
    eye = lax.broadcasted_iota(jnp.int32, (rows, rows), 0) == lax.broadcasted_iota(
        jnp.int32, (rows, rows), 1
    )
    for p in range(n):
        for q in range(n):
            line = f2[p, q : q + 1, :].astype(F32)
            w[q * rows : (q + 1) * rows, p * rows : (p + 1) * rows] = jnp.where(
                eye, line, 0.0
            ).astype(BF16)

    own_in.wait()
    for copy in sends_in:
        copy.wait_recv()

    part[...] = jnp.zeros_like(part)
    for d in range(docs):
        size = jnp.full((1, chan), counts[doc_start + d], jnp.int32).astype(F32) * blk
        scale[d : d + 1, :] = 1.0 / jnp.sqrt(size)
    for i, (d, start, width) in enumerate(pieces):
        count = counts[doc_start + d]
        lanes = pl.ds(start, width)
        if start == 0:

            @pl.loop(0, n)
            def _(q):
                here = pl.ds(pl.multiple_of(q * rows, rows), rows)
                grid = inps[d, here, :].astype(F32) * (q < count).astype(F32)
                gates[here, :] = 1.0 / (1.0 + jnp.exp(-(gain[...] * grid + bias[...])))

        for copy in sends_val[i * (n - 1) : (i + 1) * (n - 1)]:
            copy.wait_recv()

        @pl.loop(0, n // 2)
        def _(pair):
            two = pl.ds(pl.multiple_of(pair * 2 * rows, 2 * rows), 2 * rows)
            second = jnp.dot(w[two, :], vals[d, :, lanes], preferred_element_type=F32)
            full = second * gates[two, lanes]
            gated[d, two, lanes] = full.astype(BF16)
            for h in range(2):
                keep = (pair * 2 + h < count).astype(F32)
                line = jnp.sum(full[h * rows : (h + 1) * rows], axis=0, keepdims=True)
                part[d : d + 1, lanes] += line * keep

    small = []
    for k in range(1, n):
        copy = pltpu.make_async_remote_copy(
            src_ref=part,
            dst_ref=pbuf.at[me],
            send_sem=psend.at[k],
            recv_sem=precv.at[k],
            device_id={"seq": peer(k)},
            device_id_type=MESH,
        )
        copy.start()
        small.append(copy)
    pbuf[me] = part[...]
    for copy in sends_in + sends_val:
        copy.wait_send()
    for copy in small:
        copy.wait_recv()
    total = pbuf[0]
    for p in range(1, n):
        total = total + pbuf[p]
    gbuf[my_doc] = total * scale[...]
    for k in range(1, m):
        copy = pltpu.make_async_remote_copy(
            src_ref=gbuf.at[my_doc],
            dst_ref=gbuf.at[my_doc],
            send_sem=gsend.at[k],
            recv_sem=grecv.at[k],
            device_id={"doc": doc_peer(k)},
            device_id_type=MESH,
        )
        copy.start()
        small.append(copy)
    for copy in small[n - 1 :]:
        copy.wait_recv()
    for copy in small:
        copy.wait_send()


def finish_kernel(held, pooled, partner_hbm, reading_hbm, gated, contrast, reading, partner, sem):
    m, docs, chan = pooled.shape
    write = pltpu.make_async_copy(held, gated, sem.at[0])
    write.start()
    load_partner = pltpu.make_async_copy(partner_hbm, partner, sem.at[1])
    load_partner.start()
    load = pltpu.make_async_copy(reading_hbm, reading, sem.at[2])
    load.start()
    my_doc = lax.axis_index("doc")
    load_partner.wait()
    others = []
    for d in range(docs):
        want = partner[my_doc * docs + d]
        other = jnp.zeros((1, chan), F32)
        for e in range(m * docs):
            pick = (want == e).astype(F32)
            other = other + pooled[e // docs, e % docs : e % docs + 1, :] * pick
        others.append(other)
    diff = pooled[my_doc] - jnp.concatenate(others, axis=0)
    load.wait()
    contrast[...] = jnp.dot(
        diff, reading[...], precision=lax.Precision.HIGHEST, preferred_element_type=F32
    )
    write.wait()


def fused(n, m, tokens, factor_one, factor_two, gate_gain, gate_bias, block_counts, partner, reading):
    docs, blk, chan = tokens.shape
    dirs = reading.shape[1]
    smem = pl.BlockSpec(memory_space=pltpu.SMEM)
    vmem = pl.BlockSpec(memory_space=pltpu.VMEM)
    hbm = pl.BlockSpec(memory_space=pl.ANY)
    dma = pltpu.SemaphoreType.DMA
    rows = blk // n
    gated, pooled = pl.pallas_call(
        functools.partial(mixer_kernel, n, m),
        out_shape=(
            pltpu.VMEM((docs, blk, chan), BF16),
            pltpu.VMEM((m, docs, chan), F32),
        ),
        in_specs=[smem, hbm, hbm, hbm, hbm, hbm],
        out_specs=(vmem, vmem),
        scratch_shapes=[
            pltpu.VMEM((docs, blk, chan), BF16),
            pltpu.VMEM((blk, blk), BF16),
            pltpu.VMEM((docs, blk, chan), BF16),
            pltpu.VMEM((docs, blk, chan), BF16),
            pltpu.VMEM((docs, blk, chan), BF16),
            pltpu.VMEM((blk, blk), BF16),
            pltpu.VMEM((docs, chan), F32),
            pltpu.VMEM((n, docs, chan), F32),
            pltpu.VMEM((blk, chan), F32),
            pltpu.VMEM((docs, chan), F32),
            pltpu.VMEM((n, n, rows), BF16),
            pltpu.VMEM((1, chan), F32),
            pltpu.VMEM((1, chan), F32),
            dma((6,)),
            dma((n,)),
            dma((n,)),
            dma((docs + 1, n)),
            dma((docs + 1, n)),
            dma((n,)),
            dma((n,)),
            dma((m,)),
            dma((m,)),
        ],
        compiler_params=pltpu.CompilerParams(
            collective_id=0, has_side_effects=True, vmem_limit_bytes=56 << 20
        ),
        name="mixer",
    )(
        block_counts,
        tokens,
        factor_one,
        jnp.transpose(factor_two, (1, 2, 0)),
        gate_gain[None, :],
        gate_bias[None, :],
    )
    gated, contrast = pl.pallas_call(
        finish_kernel,
        out_shape=(
            jax.ShapeDtypeStruct((docs, blk, chan), BF16),
            jax.ShapeDtypeStruct((docs, dirs), F32),
        ),
        in_specs=[vmem, vmem, hbm, hbm],
        out_specs=(hbm, vmem),
        scratch_shapes=[
            pltpu.VMEM((chan, dirs), F32),
            pltpu.SMEM(partner.shape, jnp.int32),
            dma((3,)),
        ],
        compiler_params=pltpu.CompilerParams(vmem_limit_bytes=16 << 20),
        name="finish",
    )(gated, pooled, partner, reading)
    return gated.reshape(docs, n, rows, chan), contrast


def plain(tokens, factor_one, factor_two, gate_gain, gate_bias, block_counts, partner, reading):
    doc_dev, _, chan = tokens.shape
    blocks_dev, blk_size = (factor_one.shape[0], factor_one.shape[1])
    all_blocks = factor_two.shape[1]
    all_docs = block_counts.shape[0]
    doc_start = lax.axis_index("doc") * doc_dev
    block_start = lax.axis_index("seq") * blocks_dev
    local_counts = lax.dynamic_slice_in_dim(block_counts, doc_start, doc_dev)
    block_ids = block_start + jnp.arange(blocks_dev, dtype=jnp.int32)
    inside = (block_ids[None, :] < local_counts[:, None]).astype(BF16)
    grid = tokens.reshape(doc_dev, blocks_dev, blk_size, chan) * inside[:, :, None, None]
    mixed = jnp.einsum("dbic,bij->dbjc", grid, factor_one, preferred_element_type=F32).astype(BF16)
    values_t = lax.all_to_all(mixed, "seq", split_axis=2, concat_axis=1, tiled=True)
    inputs_t = lax.all_to_all(grid, "seq", split_axis=2, concat_axis=1, tiled=True)
    second = jnp.einsum("dpjc,jpq->dqjc", values_t, factor_two, preferred_element_type=F32)
    full = second * jax.nn.sigmoid(gate_gain * inputs_t.astype(F32) + gate_bias)
    keep = (jnp.arange(all_blocks, dtype=jnp.int32)[None, :] < local_counts[:, None]).astype(F32)
    partial_value = jnp.sum(full * keep[:, :, None, None], axis=(1, 2))
    scale = 1.0 / jnp.sqrt(local_counts.astype(F32) * blk_size)
    mine = lax.psum(partial_value, "seq") * scale[:, None]
    pooled_all = lax.all_gather(mine, "doc", axis=0, tiled=True)
    local_partner = lax.dynamic_slice_in_dim(partner, doc_start, doc_dev)
    picker = (local_partner[:, None] == jnp.arange(all_docs, dtype=jnp.int32)[None, :]).astype(F32)
    other = jnp.dot(picker, pooled_all, precision=lax.Precision.HIGHEST)
    contrast = jnp.dot(mine - other, reading, precision=lax.Precision.HIGHEST)
    return full.astype(BF16), contrast


def solution(mesh):
    n, m = mesh.shape["seq"], mesh.shape["doc"]

    def shards(*args):
        factor_one, factor_two = args[1], args[2]
        lanes = factor_two.shape[0] % 128 == 0
        if factor_one.shape[0] == 1 and factor_two.shape[1] == n and n % 2 == 0 and lanes:
            return fused(n, m, *args)
        return plain(*args)

    placed = (
        P("doc", "seq", None),
        P("seq", None, None),
        P("seq", None, None),
        P(),
        P(),
        P(),
        P(),
        P(),
    )
    return jax.shard_map(
        shards,
        mesh=mesh,
        in_specs=placed,
        out_specs=(P("doc", None, "seq", None), P("doc", None)),
        check_vma=False,
    )
```
